32 devices in a mesh: groups: 1, ctx: 32 (over z, y, x, core).
Axes of the slice: x: 2, y: 2, z: 4, core: 2. Of those that a mesh axis runs over, the one named last changes fastest.
Arguments:
- queries: bfloat16 [8192, 2048], P(('groups', 'ctx')), may hold values from -6 to 6
- keys: bfloat16 [8192, 1024], P(('groups', 'ctx')), may hold values from -6 to 6
- values: bfloat16 [8192, 1024], P(('groups', 'ctx')), may hold values from -6 to 6
- out_grad: bfloat16 [8192, 2048], P(('groups', 'ctx')), may hold values from -96 to 96
- q_gain: float32 [128], replicated, may hold values from 0.25 to 1.75
- k_gain: float32 [128], replicated, may hold values from 0.25 to 1.75
- doc_ids: int32 [128], P(('groups', 'ctx')), may hold values from 0 to 7, never falling along the last dimension, each value on 1 to 48 neighbouring positions
Outputs:
- query_grad: bfloat16 [8192, 2048], P(('groups', 'ctx'))
- key_grad: bfloat16 [8192, 1024], P(('groups', 'ctx'))
- value_grad: bfloat16 [8192, 1024], P(('groups', 'ctx'))
The draws below stay inside these ranges and needn't reach their ends.
Inputs may be any that keep to these rules, and one draw needn't show every extreme that they name: `doc_ids`: document ids never fall along the sequence; each document covers 1 to 48 whole blocks, and one covers exactly 48.
All inputs are finite; a program needn't handle non-finite values.
Results may differ from the reference program's by a relative error of at most 0.0075.
Values may be sent and summed in bfloat16 or wider, within the bound.
A program may use at most 128 MiB of HBM per device.

```python
import math
import jax
import jax.numpy as jnp
import numpy as np
from jax import lax

QH = 16
KVH = 8
HD = 128
WINDOW = 1024
BLK = 64
TOK_DEV = 256
SEQ = 8192
NB = 128
DOCS = 8
MOST_BLK = 48


def shard_levels(stream_key, dims, cuts, low, largest):
    def one(position, shards_of):
        draws = jax.random.uniform(jax.random.fold_in(jax.random.fold_in(stream_key, 6), position), (shards_of,), jnp.float32, low / len(cuts), largest / len(cuts))
        return jnp.repeat(jnp.exp(draws), dims[position] // shards_of).reshape((-1,) + (1,) * (len(dims) - position - 1))

    loudness = one(*cuts[0])
    for cut in cuts[1:]:
        loudness = loudness * one(*cut)
    return loudness


def length_profile(count, total, most, lean):
    weights = [(1 << 20) // math.isqrt(rank ** lean) + 1 for rank in range(2, count + 1)]
    rest, counts = total - most - (count - 1), [1] * (count - 1)
    while rest > 0:
        candidates = [i for i in range(count - 1) if counts[i] < most]
        pool, remaining = sum([weights[i] for i in candidates]), rest
        for i in candidates:
            extra = min(most - counts[i], max(1, remaining * weights[i] // pool), rest)
            counts[i] = counts[i] + extra
            rest = rest - extra
    return np.array([most] + counts)


def ragged_sizes(key, number_of, total, most, lean):
    if number_of == 2:
        one = jax.random.randint(key, (), max(1, total - most), min(most, total - 1) + 1)
        return jnp.stack([one, total - one])
    lengths = jnp.asarray(length_profile(number_of, total, most, lean), jnp.int32)
    twos = (number_of - 1) // 2
    giver, sink = lengths[1:1 + 2 * twos:2], lengths[2:2 + 2 * twos:2]
    room = jnp.minimum(giver - 1, most - sink)
    passed = jax.random.randint(jax.random.fold_in(key, 1), (twos,), 0, 1 << 20) % (room + 1)
    lengths = lengths.at[1:1 + 2 * twos:2].set(giver - passed).at[2:2 + 2 * twos:2].set(sink + passed)
    return lengths[jax.random.permutation(jax.random.fold_in(key, 2), number_of)]


def bell_draw(stream_key, shape, scale, most, shards=(), held_as=jnp.bfloat16):
    values = jax.random.normal(stream_key, shape, jnp.float32) * scale
    if len(shards) > 0:
        values = shard_levels(stream_key, shape, shards, -0.22, 0.18) * values
    return jnp.clip(values, min=-most, max=most).astype(held_as)


def setup_inputs(seed: int = 0, part: int = 0) -> dict:
    arg_keys = jax.random.split(jax.random.key(seed), 8)
    own_keys = jax.random.split(jax.random.fold_in(arg_keys[7], part), 8)
    queries = bell_draw(own_keys[0], (SEQ, QH * HD), 1.0, 6.0, ((0, 32),))
    keys = bell_draw(own_keys[1], (SEQ, KVH * HD), 1.0, 6.0, ((0, 32),))
    values = bell_draw(own_keys[2], (SEQ, KVH * HD), 1.0, 6.0, ((0, 32),))
    out_grad = bell_draw(own_keys[3], (SEQ, QH * HD), 16.0, 96.0, ((0, 32),))
    q_gain = jnp.clip(1.0 + 0.15 * jax.random.normal(arg_keys[4], (HD,), jnp.float32), 0.25, 1.75)
    k_gain = jnp.clip(1.0 + 0.15 * jax.random.normal(arg_keys[5], (HD,), jnp.float32), 0.25, 1.75)
    doc_ids = jnp.searchsorted(jnp.cumsum(ragged_sizes(own_keys[6], DOCS, NB, MOST_BLK, 2)), jnp.arange(NB), side="right").astype(jnp.int32)
    return dict(queries=queries, keys=keys, values=values, out_grad=out_grad, q_gain=q_gain, k_gain=k_gain, doc_ids=doc_ids)


qk_scale = 168.0 ** (-0.5)
norm_epsilon = 1e-06

def rms_norm(values_in, gain):
    inverse_rms = lax.rsqrt(lax.optimization_barrier(jnp.mean(values_in * values_in, axis=-1, keepdims=True)) + norm_epsilon)
    return (values_in * inverse_rms * gain, inverse_rms)

def rms_norm_back(values_in, inverse_rms, gain, incoming):
    scaled = incoming * gain
    cubed = inverse_rms * inverse_rms * inverse_rms
    return inverse_rms * scaled - values_in * cubed * lax.optimization_barrier(jnp.mean(values_in * scaled, axis=-1, keepdims=True))

def tile_mask(offset_rows, query_docs, key_docs, usable):
    count_rows = query_docs.shape[0]
    spacing = offset_rows + jnp.arange(count_rows, dtype=jnp.int32)[:, None] - jnp.arange(count_rows, dtype=jnp.int32)[None, :]
    return (spacing >= 0) & (spacing < WINDOW) & (query_docs[:, None] == key_docs[None, :]) & usable

def halfway_round(values_in):
    return lax.optimization_barrier(values_in.astype(jnp.bfloat16)).astype(jnp.float32)

def forward_tile(query_tile_rows, key_tile_rows, value_tile_rows, key_mask):
    score_matrix = jnp.einsum('jefo,heo->efjh', query_tile_rows.astype(jnp.float32), key_tile_rows.astype(jnp.float32))
    attention_weight = jnp.where(key_mask, jnp.exp(score_matrix), 0.0)
    totals = lax.optimization_barrier(jnp.sum(attention_weight, axis=-1))
    reduced_total = jnp.einsum('jleq,qjn->ejln', halfway_round(attention_weight), value_tile_rows.astype(jnp.float32))
    return (totals, reduced_total)

def backward_tile(query_tile_rows, key_tile_rows, value_tile_rows, gradient_tile_rows, key_mask, totals, deltas):
    score_matrix = jnp.einsum('jefo,heo->efjh', query_tile_rows.astype(jnp.float32), key_tile_rows.astype(jnp.float32))
    attention_weight = jnp.where(key_mask, jnp.exp(score_matrix), 0.0)
    probability_rows = attention_weight / totals[..., None]
    value_section = jnp.einsum('xqpt,pxqh->txh', halfway_round(probability_rows), gradient_tile_rows.astype(jnp.float32))
    probability_gradient = jnp.einsum('jefo,heo->efjh', gradient_tile_rows.astype(jnp.float32), value_tile_rows.astype(jnp.float32))
    score_gradient = halfway_round(probability_rows * (probability_gradient - deltas[..., None]))
    query_section = jnp.einsum('jleq,qjn->ejln', score_gradient, key_tile_rows.astype(jnp.float32))
    key_section = jnp.einsum('xqpt,pxqh->txh', score_gradient, query_tile_rows.astype(jnp.float32))
    return (query_section, key_section, value_section)

def reference(queries, keys, values, out_grad, q_gain, k_gain, doc_ids):
    block_rows = TOK_DEV
    reach = WINDOW // block_rows
    total_rows = queries.shape[0]
    block_count = total_rows // block_rows
    kv_heads = keys.shape[1] // HD
    group_size = queries.shape[1] // keys.shape[1]
    q_raw = queries.astype(jnp.float32).reshape(total_rows, kv_heads, group_size, HD)
    q_normed, q_inverse = rms_norm(q_raw, q_gain * qk_scale)
    q_half = q_normed.astype(jnp.bfloat16)
    k_raw = keys.astype(jnp.float32).reshape(total_rows, kv_heads, HD)
    k_normed, k_inverse = rms_norm(k_raw, k_gain)
    k_half = k_normed.astype(jnp.bfloat16)
    v_half = values.reshape(total_rows, kv_heads, HD)
    grad_half = out_grad.reshape(total_rows, kv_heads, group_size, HD)
    token_docs = jnp.repeat(doc_ids, BLK)
    padding = reach * block_rows
    k_padded = jnp.concatenate([jnp.zeros((padding, kv_heads, HD), jnp.bfloat16), k_half], axis=0)
    v_padded = jnp.concatenate([jnp.zeros((padding, kv_heads, HD), jnp.bfloat16), v_half], axis=0)
    docs_padded = jnp.concatenate([jnp.full((padding,), -1, jnp.int32), token_docs.astype(jnp.int32)], axis=0)

    def one_block(carry, block_index):
        key_acc, value_acc = carry
        start = block_index * block_rows
        query_tile_rows = lax.dynamic_slice_in_dim(q_half, start, block_rows, 0)
        gradient_tile_rows = lax.dynamic_slice_in_dim(grad_half, start, block_rows, 0)
        query_docs = lax.dynamic_slice_in_dim(token_docs, start, block_rows, 0)
        pieces = []
        for distance in range(reach + 1):
            key_start = start + (reach - distance) * block_rows
            key_tile_rows = lax.dynamic_slice_in_dim(k_padded, key_start, block_rows, 0)
            value_tile_rows = lax.dynamic_slice_in_dim(v_padded, key_start, block_rows, 0)
            key_docs = lax.dynamic_slice_in_dim(docs_padded, key_start, block_rows, 0)
            key_mask = tile_mask(distance * block_rows, query_docs, key_docs, True)
            pieces.append((key_start, key_tile_rows, value_tile_rows, key_mask))
        totals = jnp.zeros((kv_heads, group_size, block_rows), jnp.float32)
        reduced_total = jnp.zeros((block_rows, kv_heads, group_size, HD), jnp.float32)
        for key_start, key_tile_rows, value_tile_rows, key_mask in pieces:
            tile_totals, tile_summed = forward_tile(query_tile_rows, key_tile_rows, value_tile_rows, key_mask)
            totals = totals + tile_totals
            reduced_total = reduced_total + tile_summed
        outputs = reduced_total / jnp.transpose(totals, (2, 0, 1))[..., None]
        deltas = jnp.transpose(lax.optimization_barrier(jnp.sum(gradient_tile_rows.astype(jnp.float32) * outputs, axis=-1)), (1, 2, 0))
        query_acc = jnp.zeros((block_rows, kv_heads, group_size, HD), jnp.float32)
        for key_start, key_tile_rows, value_tile_rows, key_mask in pieces:
            query_section, key_section, value_section = backward_tile(query_tile_rows, key_tile_rows, value_tile_rows, gradient_tile_rows, key_mask, totals, deltas)
            query_acc = query_acc + query_section
            key_now = lax.dynamic_slice_in_dim(key_acc, key_start, block_rows, 0)
            key_acc = lax.dynamic_update_slice_in_dim(key_acc, key_now + key_section, key_start, 0)
            value_now = lax.dynamic_slice_in_dim(value_acc, key_start, block_rows, 0)
            value_acc = lax.dynamic_update_slice_in_dim(value_acc, value_now + value_section, key_start, 0)
        q_raw_block = lax.dynamic_slice_in_dim(q_raw, start, block_rows, 0)
        q_inverse_block = lax.dynamic_slice_in_dim(q_inverse, start, block_rows, 0)
        query_out = rms_norm_back(q_raw_block, q_inverse_block, q_gain * qk_scale, query_acc).astype(jnp.bfloat16)
        return ((key_acc, value_acc), query_out)
    empty = jnp.zeros((padding + total_rows, kv_heads, HD), jnp.float32)
    (key_acc, value_acc), query_blocks = lax.scan(one_block, (empty, empty), jnp.arange(block_count, dtype=jnp.int32))
    query_grad = query_blocks.reshape(total_rows, kv_heads * group_size * HD)
    key_grad = rms_norm_back(k_raw, k_inverse, k_gain, key_acc[padding:]).astype(jnp.bfloat16).reshape(total_rows, kv_heads * HD)
    value_grad = value_acc[padding:].astype(jnp.bfloat16).reshape(total_rows, kv_heads * HD)
    return (query_grad, key_grad, value_grad)
```

```python
import functools

import jax
import jax.numpy as jnp
from jax import lax
from jax.experimental import pallas as pl
from jax.experimental.pallas import tpu as pltpu
from jax.sharding import PartitionSpec as P

HD = 128
WINDOW = 1024
BLK = 64

qk_scale = 168.0 ** (-0.5)
norm_epsilon = 1e-06

F32 = jnp.float32
BF16 = jnp.bfloat16


def dot(a, b, contract):
    return lax.dot_general(
        a, b, (((contract[0],), (contract[1],)), ((), ())), preferred_element_type=F32
    )


def inverse_rms(x):
    return lax.rsqrt(jnp.mean(x * x, axis=-1, keepdims=True) + norm_epsilon)


def norm_back(x, r, gain, incoming):
    scaled = incoming * gain
    return r * scaled - x * (r * r * r) * jnp.mean(x * scaled, axis=-1, keepdims=True)


def kernel(
    n, q_in, k_in, v_in, g_in, qgain, kgain, docs_in,
    out_q, out_k, out_v,
    qx, gx, kx, docs_own, docs, kv, kn, efar, eown, qn, gn, lsum, osum, drow, dqsum, part0, part2,
    send1, send2, recv1, recv2, dq, dkv,
    x_local, x_send, x_recv, du_send, du_recv, dx_send, dx_recv,
    up_send, up_recv, xn_send, xn_recv,
    g1_send, g1_recv, g2_send, g2_recv,
    fq_local, fq_send, fq_recv, fk_local, fk_send, fk_recv,
):
    T = q_in.shape[0]
    HH = kv.shape[1]
    G = q_in.shape[1] // k_in.shape[1]
    QW = HH * G * HD
    KW = HH * HD
    C = 2 * T
    per = WINDOW // T + 1

    me = lax.axis_index("ctx")
    core = lax.rem(me, 2)
    other = 1 - core
    chip = me // 2
    par = lax.rem(chip, 2)
    partner = me + 1 - 2 * core
    xn = me + 2 - 4 * par
    has_up, has_down = chip < n // 2 - 2, chip >= 2
    up = lax.rem(me + 4, n)
    down = lax.rem(me + n - 4, n)

    barrier = pltpu.get_barrier_semaphore()
    flip = 1 - 2 * core
    for who in (partner, xn, xn + flip, up, up + flip, down, down + flip):
        pl.semaphore_signal(
            barrier, inc=1, device_id={"ctx": who}, device_id_type=pl.DeviceIdType.MESH
        )

    def remote(src, dst, s, r, who):
        return pltpu.make_async_remote_copy(
            src_ref=src, dst_ref=dst, send_sem=s, recv_sem=r,
            device_id={"ctx": who}, device_id_type=pl.DeviceIdType.MESH,
        )

    def half(c):
        return pl.ds(pl.multiple_of(c * T, T), T)

    rows = half(core)
    for b in range(docs_in.shape[0]):
        docs_own[b : b + 1, :] = jnp.full((1, HD), docs_in[b], jnp.int32)

    def part(who, width, at=0, size=None):
        size = width if size is None else size
        return pl.ds(pl.multiple_of(who * width + at, size), size)

    def swap(src, dst, i, mine, theirs):
        rc = remote(src.at[:, theirs], dst, x_send.at[i], x_recv.at[i], partner)
        lc = pltpu.make_async_copy(src.at[:, mine], dst, x_local.at[i])
        return rc, lc

    swaps = [
        swap(k_in, kx.at[rows, :], 0, part(core, KW), part(other, KW)),
        swap(q_in, qx.at[rows, :], 1, part(core, QW), part(other, QW)),
        swap(g_in, gx.at[rows, :], 2, part(core, QW), part(other, QW)),
        (
            remote(docs_own, docs.at[0, core], x_send.at[3], x_recv.at[3], partner),
            pltpu.make_async_copy(docs_own, docs.at[0, core], x_local.at[3]),
        ),
    ] + [
        swap(
            v_in, kv.at[0, h, 1, rows, :], 4 + h,
            part(core, KW, h * HD, HD), part(other, KW, h * HD, HD),
        )
        for h in range(HH)
    ]
    order = (3, 0, 4, 1, 5, 6, 7, 2) if HH == 4 else tuple(range(len(swaps)))

    def arrived(i):
        swaps[i][0].wait_recv()
        swaps[i][1].wait()

    def reach(who, c):
        return who + (c - core)

    def to_up(h, w, j, s):
        src = (k_in, v_in)[w].at[:, part(j, KW, h * HD, HD)]
        return remote(
            src, kv.at[2, h, w, half(s), :], up_send.at[h, w, j], up_recv.at[h, w, s],
            reach(up, j),
        )

    def to_xn(h, w, j, s):
        src = (k_in, v_in)[w].at[:, part(j, KW, h * HD, HD)]
        return remote(
            src, kv.at[1, h, w, half(s), :], xn_send.at[h, w, j], xn_recv.at[h, w, s],
            reach(xn, j),
        )

    def relay(h, w, s):
        return remote(
            kv.at[2, h, w, half(s), :], kv.at[1, h, w, half(s), :],
            xn_send.at[h, w, s], xn_recv.at[h, w, s], xn,
        )

    def doc_up(j, s):
        return remote(docs_own, docs.at[2, s], du_send.at[j], du_recv.at[s], reach(up, j))

    def doc_xn(j, s):
        return remote(docs_own, docs.at[1, s], dx_send.at[j], dx_recv.at[s], reach(xn, j))

    def doc_relay(s):
        return remote(docs.at[2, s], docs.at[1, s], dx_send.at[s], dx_recv.at[s], xn)

    for i in order:
        swaps[i][1].start()

    pl.semaphore_wait(barrier, 7)

    both = (core, other)
    swaps[3][0].start()

    @pl.when(has_up)
    def _():
        for j in both:
            doc_up(j, core).start()

    @pl.when(par == 0)
    def _():
        for j in both:
            doc_xn(j, core).start()

    for h in range(HH):

        @pl.when(has_up)
        def _():
            for w in range(2):
                for j in both:
                    to_up(h, w, j, core).start()

        @pl.when(par == 0)
        def _():
            for w in range(2):
                for j in both:
                    to_xn(h, w, j, core).start()

    for i in order[1:]:
        swaps[i][0].start()

    @pl.when(chip < 2)
    def _():
        kv[2] = jnp.zeros(kv.shape[1:], BF16)
        docs[2] = jnp.zeros(docs.shape[1:], jnp.int32)

    @pl.when(chip >= n // 2 - 2)
    def _():
        recv2[...] = jnp.zeros(recv2.shape, BF16)

    arrived(3)
    for s in both:

        @pl.when(has_down)
        def _():
            doc_up(s, s).wait_recv()

        @pl.when(par == 1)
        def _():
            doc_relay(s).start()

    arrived(0)

    for h in range(HH):
        x = kx[:, h * HD : (h + 1) * HD].astype(F32)
        kv[0, h, 0] = (x * inverse_rms(x) * kgain[...]).astype(BF16)

    for s in range(2):
        doc_xn(s, s).wait_recv()

    lane = lax.broadcasted_iota(jnp.int32, (1, HD), 1)
    blocks = T // BLK
    qdocs = []
    for m in range(2):
        for b in range(0, blocks, 2):
            qdocs.append(
                jnp.where(lane < BLK, docs[0, m, b : b + 1, :], docs[0, m, b + 1 : b + 2, :])
            )
    lows = []
    for i, qd in enumerate(qdocs):
        low = jnp.zeros((1, HD), jnp.int32)
        for slot in (2, 1, 0):
            for m in range(2):
                for b in range(blocks):
                    kd = jnp.where(chip >= slot, docs[slot, m, b : b + 1, :], -1)
                    low = low + jnp.where(kd < qd, BLK, 0)
        lows.append(jnp.maximum(low, lane + (i * HD + 1)))
    hl = len(lows) // 2
    low_rows = [
        jnp.concatenate([x for _ in range(G) for x in lows[t * hl : (t + 1) * hl]], axis=1)
        for t in range(2)
    ]
    tile_rows = lax.broadcasted_iota(jnp.int32, (T, G * T), 0)
    tile_cols = lax.broadcasted_iota(jnp.int32, (T, G * T), 1)
    causal = tile_rows <= lax.rem(tile_cols, T)

    arrived(1)
    for h in range(HH):
        arrived(4 + h)

    def key_tile(h, which, b):
        slot, r = 2 - b // 2, b % 2
        if which == 0 and slot > 0:
            return kn[slot - 1, r * T : (r + 1) * T, :]
        return kv[slot, h, which, r * T : (r + 1) * T, :]

    def take_up(h, w):
        for s in both:

            @pl.when(has_down)
            def _():
                to_up(h, w, s, s).wait_recv()

            @pl.when(par == 1)
            def _():
                relay(h, w, s).start()

    def g1(h, w):
        return remote(
            send1.at[h, w], recv1.at[h, w], g1_send.at[h, w], g1_recv.at[h, w], xn
        )

    def g2(h, w):
        return remote(
            send2.at[h, w], recv2.at[h, w], g2_send.at[h, w], g2_recv.at[h, w], down
        )

    def pass_down(h, w):
        @pl.when(par == 1)
        def _():
            g1(h, w).wait_recv()
            send2[h, w] = (part2[h, w] + recv1[h, w].astype(F32)).astype(BF16)

            @pl.when(has_down)
            def _():
                g2(h, w).start()

    def fq(h):
        cols = pl.ds(pl.multiple_of(h * (G * HD), G * HD), G * HD)
        to = pl.ds(pl.multiple_of(core * QW + h * (G * HD), G * HD), G * HD)
        return (
            remote(dq.at[other, :, cols], out_q.at[:, to], fq_send.at[h], fq_recv.at[h], partner),
            pltpu.make_async_copy(dq.at[core, :, cols], out_q.at[:, to], fq_local.at[h]),
        )

    def fk(h):
        cols = pl.ds(pl.multiple_of(h * HD, HD), HD)
        to = pl.ds(pl.multiple_of(core * KW + h * HD, HD), HD)
        pairs = []
        for w, out in ((0, out_k), (1, out_v)):
            pairs.append((
                remote(dkv.at[w, other, :, cols], out.at[:, to], fk_send.at[w, h],
                       fk_recv.at[w, h], partner),
                pltpu.make_async_copy(dkv.at[w, core, :, cols], out.at[:, to], fk_local.at[w, h]),
            ))
        return pairs

    qg = qgain[...] * qk_scale
    own_at = {(0, 4): 0, (1, 4): 1, (1, 5): 2}

    def head_cols(h, g):
        return pl.ds(pl.multiple_of((h * G + g) * HD, HD), HD)

    def forward(h, t, b, q):
        s = dot(key_tile(h, 0, b), q, (1, 1))
        seen = tile_rows >= low_rows[t] - b * T
        if b == t + per - 1:
            seen = seen & causal
        e = jnp.where(seen, jnp.exp(s), 0.0)
        eb = e.astype(BF16)
        return eb, jnp.sum(e, axis=0, keepdims=True), dot(key_tile(h, 1, b), eb, (0, 0))

    def backward(h, b, ebs):
        dk = dv = None
        terms = {}
        for t, eb in ebs.items():
            dp = dot(key_tile(h, 1, b), gn[h, t], (1, 1))
            ds = (eb.astype(F32) * (dp - drow[h, t])).astype(BF16)
            dv_t = dot(eb, gn[h, t], (1, 0))
            dk_t = dot(ds, qn[h, t], (1, 0))
            dk = dk_t if dk is None else dk + dk_t
            dv = dv_t if dv is None else dv + dv_t
            terms[t] = dot(key_tile(h, 0, b), ds, (0, 0))
        return dk, dv, terms

    def own_forward(h, carry):
        for t in range(2):
            qn[h, t] = jnp.concatenate(
                [
                    (x * inverse_rms(x) * qg).astype(BF16)
                    for x in (
                        qx[t * T : (t + 1) * T, head_cols(h, g)].astype(F32) for g in range(G)
                    )
                ],
                axis=0,
            )
            total, o_t = 0.0, 0.0
            for b in (4, 5)[: t + 1]:
                eb, part, o_part = forward(h, t, b, qn[h, t])
                eown[h, own_at[t, b]] = eb
                total, o_t = total + part, o_t + o_part
            lsum[h, t] = total
            osum[h, t] = o_t

        for w in range(2):

            @pl.when(h == 2 * w)
            def _():
                take_up(0, w)

        return carry

    lax.fori_loop(0, HH, own_forward, 0)
    arrived(2)

    def head(h, carry):
        for w in range(2):
            for s in range(2):
                relay(h, w, s).wait_recv()
        for slot in (1, 2):
            x = kv[slot, h, 0].astype(F32)
            kn[slot - 1] = (x * inverse_rms(x) * kgain[...]).astype(BF16)
        for t in range(2):
            total, o_t = lsum[h, t], osum[h, t]
            for b in range(t, 4):
                eb, part, o_part = forward(h, t, b, qn[h, t])
                efar[t, b] = eb
                total, o_t = total + part, o_t + o_part
            inv = 1.0 / total
            grads = [gx[t * T : (t + 1) * T, head_cols(h, g)].astype(F32) for g in range(G)]
            g_t = jnp.concatenate(grads, axis=0).T * inv
            drow[h, t] = jnp.sum(g_t.astype(BF16).astype(F32) * o_t, axis=0, keepdims=True) * inv
            gn[h, t] = g_t.T.astype(BF16)

        @pl.when(h + 1 < HH)
        def _():
            take_up(h + 1, 0)

        dq_t = [0.0, 0.0]
        for b in (2, 3):
            dk, dv, terms = backward(h, b, {t: efar[t, b] for t in range(2)})
            at = slice((b - 2) * T, (b - 1) * T)
            send1[h, 0, at] = dk.astype(BF16)
            send1[h, 1, at] = dv.astype(BF16)
            for t in terms:
                dq_t[t] = dq_t[t] + terms[t]

        @pl.when((par == 0) | (h == HH - 1))
        def _():
            for w in range(2):
                g1(h, w).start()

        @pl.when(h + 1 < HH)
        def _():
            take_up(h + 1, 1)

        @pl.when((par == 1) & (h == HH - 2))
        def _():
            for i in range(HH - 1):
                for w in range(2):
                    g1(i, w).start()

        for b in (0, 1):
            dk, dv, terms = backward(h, b, {t: efar[t, b] for t in range(b + 1)})
            at = slice(b * T, (b + 1) * T)
            part2[h, 0, at] = dk
            part2[h, 1, at] = dv
            for t in terms:
                dq_t[t] = dq_t[t] + terms[t]
        for t in range(2):
            dqsum[h, t] = dq_t[t]

        @pl.when((par == 0) & has_down)
        def _():
            for w in range(2):
                send2[h, w] = part2[h, w].astype(BF16)

            @pl.when(h == HH - 2)
            def _():
                for i in range(HH - 1):
                    for w in range(2):
                        g2(i, w).start()

            @pl.when(h == HH - 1)
            def _():
                for w in range(2):
                    g2(h, w).start()

        @pl.when(h == HH - 1)
        def _():
            for w in range(2):
                pass_down(0, w)

        return carry

    lax.fori_loop(0, HH, head, 0)

    def own_backward(h, carry):
        dq_t = [dqsum[h, 0], dqsum[h, 1]]
        for b in (4, 5):
            dk, dv, terms = backward(
                h, b, {t: eown[h, own_at[t, b]] for t in range(b - 4, 2)}
            )
            at = slice((b - 4) * T, (b - 3) * T)
            part0[h, 0, at] = dk
            part0[h, 1, at] = dv
            for t in terms:
                dq_t[t] = dq_t[t] + terms[t]
        for t in range(2):
            dqn = dq_t[t].T
            for g in range(G):
                x = qx[t * T : (t + 1) * T, head_cols(h, g)].astype(F32)
                dq[t, :, head_cols(h, g)] = norm_back(
                    x, inverse_rms(x), qg, dqn[g * T : (g + 1) * T]
                ).astype(BF16)
        far, near = fq(h)
        far.start()
        near.start()

        for w in range(2):

            @pl.when(h == 1 + w)
            def _():
                pass_down(1, w)

        return carry

    lax.fori_loop(0, HH, own_backward, 0)
    for i in range(2, HH):
        for w in range(2):
            pass_down(i, w)

    def finish(h, carry):
        cols = pl.ds(pl.multiple_of(h * HD, HD), HD)
        @pl.when(has_up)
        def _():
            for w in range(2):
                g2(h, w).wait_recv()

        @pl.when(par == 0)
        def _():
            for w in range(2):
                g1(h, w).wait_recv()

        own = part0[h] + recv2[h].astype(F32)
        own = own + jnp.where(par == 0, recv1[h].astype(F32), 0.0)
        x = kx[:, cols].astype(F32)
        dk = norm_back(x, inverse_rms(x), kgain[...], own[0]).astype(BF16)
        dv = own[1].astype(BF16)
        for m in range(2):
            dkv[0, m, :, cols] = dk[m * T : (m + 1) * T]
            dkv[1, m, :, cols] = dv[m * T : (m + 1) * T]
        for far, near in fk(h):
            far.start()
            near.start()
        return carry

    lax.fori_loop(0, HH, finish, 0)

    for rc, lc in swaps:
        rc.wait_send()

    for s in range(2):
        doc_xn(s, s).wait_send()

        @pl.when(has_up)
        def _():
            doc_up(s, s).wait_send()

    def drain(h, carry):
        for w in range(2):
            for s in range(2):
                to_xn(h, w, s, s).wait_send()
            g1(h, w).wait_send()

        @pl.when(has_up)
        def _():
            for w in range(2):
                for s in range(2):
                    to_up(h, w, s, s).wait_send()

        @pl.when(has_down)
        def _():
            for w in range(2):
                g2(h, w).wait_send()

        for far, near in [fq(h)] + fk(h):
            far.wait_send()
            far.wait_recv()
            near.wait()
        return carry

    lax.fori_loop(0, HH, drain, 0)


def on_device(n, queries, keys, values, out_grad, q_gain, k_gain, doc_ids):
    T = queries.shape[0]
    kv_heads = keys.shape[1] // HD
    HH = kv_heads // 2
    G = queries.shape[1] // keys.shape[1]
    C = 2 * T
    per = WINDOW // T + 1
    doc_tile = (-(-doc_ids.shape[0] // 8) * 8, HD)
    DMA = pltpu.SemaphoreType.DMA
    vmem = pl.BlockSpec(memory_space=pltpu.VMEM)
    anywhere = pl.BlockSpec(memory_space=pltpu.HBM)
    scratch = [
        pltpu.VMEM((C, HH * G * HD), BF16),
        pltpu.VMEM((C, HH * G * HD), BF16),
        pltpu.VMEM((C, HH * HD), BF16),
        pltpu.VMEM(doc_tile, jnp.int32),
        pltpu.VMEM((3, 2) + doc_tile, jnp.int32),
        pltpu.VMEM((3, HH, 2, C, HD), BF16),
        pltpu.VMEM((2, C, HD), BF16),
        pltpu.VMEM((2, per - 1, T, G * T), BF16),
        pltpu.VMEM((HH, 3, T, G * T), BF16),
        pltpu.VMEM((HH, 2, G * T, HD), BF16),
        pltpu.VMEM((HH, 2, G * T, HD), BF16),
        pltpu.VMEM((HH, 2, 1, G * T), F32),
        pltpu.VMEM((HH, 2, HD, G * T), F32),
        pltpu.VMEM((HH, 2, 1, G * T), F32),
        pltpu.VMEM((HH, 2, HD, G * T), F32),
        pltpu.VMEM((HH, 2, C, HD), F32),
        pltpu.VMEM((HH, 2, C, HD), F32),
        pltpu.VMEM((HH, 2, C, HD), BF16),
        pltpu.VMEM((HH, 2, C, HD), BF16),
        pltpu.VMEM((HH, 2, C, HD), BF16),
        pltpu.VMEM((HH, 2, C, HD), BF16),
        pltpu.VMEM((2, T, HH * G * HD), BF16),
        pltpu.VMEM((2, 2, T, HH * HD), BF16),
        DMA((4 + HH,)), DMA((4 + HH,)), DMA((4 + HH,)), DMA((2,)), DMA((2,)), DMA((2,)), DMA((2,)),
        DMA((HH, 2, 2)), DMA((HH, 2, 2)), DMA((HH, 2, 2)), DMA((HH, 2, 2)),
        DMA((HH, 2)), DMA((HH, 2)), DMA((HH, 2)), DMA((HH, 2)),
        DMA((HH,)), DMA((HH,)), DMA((HH,)), DMA((2, HH)), DMA((2, HH)), DMA((2, HH)),
    ]
    return pl.pallas_call(
        functools.partial(kernel, n),
        out_shape=(
            pltpu.VMEM(queries.shape, BF16),
            pltpu.VMEM(keys.shape, BF16),
            pltpu.VMEM(values.shape, BF16),
        ),
        in_specs=[anywhere] * 4 + [vmem, vmem, pl.BlockSpec(memory_space=pltpu.SMEM)],
        out_specs=(vmem, vmem, vmem),
        scratch_shapes=scratch,
        compiler_params=pltpu.CompilerParams(
            collective_id=0, has_side_effects=True, vmem_limit_bytes=64700000
        ),
    )(queries, keys, values, out_grad, q_gain.reshape(1, HD), k_gain.reshape(1, HD), doc_ids)


def solution(mesh):
    split = P(("groups", "ctx"), None)
    return jax.shard_map(
        functools.partial(on_device, mesh.shape["ctx"]),
        mesh=mesh,
        in_specs=(split, split, split, split, P(), P(), P(("groups", "ctx"))),
        out_specs=(split, split, split),
        check_vma=False,
    )
```

```python
import functools

import jax
import jax.numpy as jnp
from jax import lax
from jax.experimental import pallas as pl
from jax.experimental.pallas import tpu as pltpu
from jax.sharding import PartitionSpec as P

HD = 128
WINDOW = 1024
BLK = 64

qk_scale = 168.0 ** (-0.5)
norm_epsilon = 1e-06

F32 = jnp.float32
BF16 = jnp.bfloat16


def dot(a, b, contract):
    return lax.dot_general(
        a, b, (((contract[0],), (contract[1],)), ((), ())), preferred_element_type=F32
    )


def inverse_rms(x):
    return lax.rsqrt(jnp.mean(x * x, axis=-1, keepdims=True) + norm_epsilon)


def norm_back(x, r, gain, incoming):
    scaled = incoming * gain
    return r * scaled - x * (r * r * r) * jnp.mean(x * scaled, axis=-1, keepdims=True)


def kernel(
    n, q_in, k_in, v_in, g_in, qgain, kgain, docs_in,
    out_q, out_k, out_v,
    qx, gx, kx, docs_own, docs, kv, kn, efar, eown, qn, gn, lsum, osum, drow, dqsum, part0, part2,
    send1, send2, recv1, recv2, dq, dkv,
    x_local, x_send, x_recv, du_send, du_recv, dx_send, dx_recv,
    up_send, up_recv, xn_send, xn_recv,
    g1_send, g1_recv, g2_send, g2_recv,
    fq_local, fq_send, fq_recv, fk_local, fk_send, fk_recv,
):
    T = q_in.shape[0]
    HH = kv.shape[1]
    G = q_in.shape[1] // k_in.shape[1]
    QW = HH * G * HD
    KW = HH * HD
    C = 2 * T
    per = WINDOW // T + 1

    me = lax.axis_index("ctx")
    core = lax.rem(me, 2)
    other = 1 - core
    chip = me // 2
    par = lax.rem(chip, 2)
    partner = me + 1 - 2 * core
    xn = me + 2 - 4 * par
    has_up, has_down = chip < n // 2 - 2, chip >= 2
    up = lax.rem(me + 4, n)
    down = lax.rem(me + n - 4, n)

    barrier = pltpu.get_barrier_semaphore()
    flip = 1 - 2 * core

    def greet(*peers):
        for who in peers:
            pl.semaphore_signal(
                barrier, inc=1, device_id={"ctx": who}, device_id_type=pl.DeviceIdType.MESH
            )

    @pl.when(has_up)
    def _():
        greet(up, up + flip)

    @pl.when(has_down)
    def _():
        greet(down, down + flip)

    greet(xn, xn + flip, partner)

    def remote(src, dst, s, r, who):
        return pltpu.make_async_remote_copy(
            src_ref=src, dst_ref=dst, send_sem=s, recv_sem=r,
            device_id={"ctx": who}, device_id_type=pl.DeviceIdType.MESH,
        )

    def half(c):
        return pl.ds(pl.multiple_of(c * T, T), T)

    rows = half(core)
    for b in range(docs_in.shape[0]):
        docs_own[b : b + 1, :] = jnp.full((1, HD), docs_in[b], jnp.int32)

    def part(who, width, at=0, size=None):
        size = width if size is None else size
        return pl.ds(pl.multiple_of(who * width + at, size), size)

    def swap(src, dst, i, mine, theirs):
        rc = remote(src.at[:, theirs], dst, x_send.at[i], x_recv.at[i], partner)
        lc = pltpu.make_async_copy(src.at[:, mine], dst, x_local.at[i])
        return rc, lc

    swaps = [
        swap(k_in, kx.at[rows, :], 0, part(core, KW), part(other, KW)),
        swap(q_in, qx.at[rows, :], 1, part(core, QW), part(other, QW)),
        swap(g_in, gx.at[rows, :], 2, part(core, QW), part(other, QW)),
        (
            remote(docs_own, docs.at[0, core], x_send.at[3], x_recv.at[3], partner),
            pltpu.make_async_copy(docs_own, docs.at[0, core], x_local.at[3]),
        ),
    ] + [
        swap(
            v_in, kv.at[0, h, 1, rows, :], 4 + h,
            part(core, KW, h * HD, HD), part(other, KW, h * HD, HD),
        )
        for h in range(HH)
    ]
    order = (3, 0, 4, 1, 5, 6, 7, 2) if HH == 4 else tuple(range(len(swaps)))

    def arrived(i):
        swaps[i][0].wait_recv()
        swaps[i][1].wait()

    def reach(who, c):
        return who + (c - core)

    def to_up(h, w, j, s):
        src = (k_in, v_in)[w].at[:, part(j, KW, h * HD, HD)]
        return remote(
            src, kv.at[2, h, w, half(s), :], up_send.at[h, w, j], up_recv.at[h, w, s],
            reach(up, j),
        )

    def to_xn(h, w, j, s):
        src = (k_in, v_in)[w].at[:, part(j, KW, h * HD, HD)]
        return remote(
            src, kv.at[1, h, w, half(s), :], xn_send.at[h, w, j], xn_recv.at[h, w, s],
            reach(xn, j),
        )

    def relay(h, w, s):
        return remote(
            kv.at[2, h, w, half(s), :], kv.at[1, h, w, half(s), :],
            xn_send.at[h, w, s], xn_recv.at[h, w, s], xn,
        )

    def doc_up(j, s):
        return remote(docs_own, docs.at[2, s], du_send.at[j], du_recv.at[s], reach(up, j))

    def doc_xn(j, s):
        return remote(docs_own, docs.at[1, s], dx_send.at[j], dx_recv.at[s], reach(xn, j))

    def doc_relay(s):
        return remote(docs.at[2, s], docs.at[1, s], dx_send.at[s], dx_recv.at[s], xn)

    for i in order:
        swaps[i][1].start()

    pl.semaphore_wait(barrier, 3 + 2 * jnp.where(has_up, 1, 0) + 2 * jnp.where(has_down, 1, 0))

    both = (core, other)
    swaps[3][0].start()

    @pl.when(has_up)
    def _():
        for j in both:
            doc_up(j, core).start()

    @pl.when(par == 0)
    def _():
        for j in both:
            doc_xn(j, core).start()

    for h in range(HH):

        @pl.when(has_up)
        def _():
            for w in range(2):
                for j in both:
                    to_up(h, w, j, core).start()

        if h < HH - 1:

            @pl.when(par == 0)
            def _():
                for w in range(2):
                    for j in both:
                        to_xn(h, w, j, core).start()

    for i in order[1:]:
        swaps[i][0].start()

    @pl.when(chip < 2)
    def _():
        kv[2] = jnp.zeros(kv.shape[1:], BF16)
        docs[2] = jnp.zeros(docs.shape[1:], jnp.int32)

    @pl.when(chip >= n // 2 - 2)
    def _():
        recv2[...] = jnp.zeros(recv2.shape, BF16)

    arrived(3)
    for s in both:

        @pl.when(has_down)
        def _():
            doc_up(s, s).wait_recv()

        @pl.when(par == 1)
        def _():
            doc_relay(s).start()

    def take_up(h, w, *sides):
        @pl.when(par == 1)
        def _():
            for s in sides:

                @pl.when(has_down)
                def _():
                    to_up(h, w, s, s).wait_recv()

                relay(h, w, s).start()

    take_up(0, 0, core)
    arrived(0)

    for h in range(HH):
        x = kx[:, h * HD : (h + 1) * HD].astype(F32)
        kv[0, h, 0] = (x * inverse_rms(x) * kgain[...]).astype(BF16)

    for s in range(2):
        doc_xn(s, s).wait_recv()

    lane = lax.broadcasted_iota(jnp.int32, (1, HD), 1)
    blocks = T // BLK
    qdocs = []
    for m in range(2):
        for b in range(0, blocks, 2):
            qdocs.append(
                jnp.where(lane < BLK, docs[0, m, b : b + 1, :], docs[0, m, b + 1 : b + 2, :])
            )
    lows = []
    for i, qd in enumerate(qdocs):
        low = jnp.zeros((1, HD), jnp.int32)
        for slot in (2, 1, 0):
            for m in range(2):
                for b in range(blocks):
                    kd = jnp.where(chip >= slot, docs[slot, m, b : b + 1, :], -1)
                    low = low + jnp.where(kd < qd, BLK, 0)
        lows.append(jnp.maximum(low, lane + (i * HD + 1)))
    hl = len(lows) // 2
    low_rows = [
        jnp.concatenate([x for _ in range(G) for x in lows[t * hl : (t + 1) * hl]], axis=1)
        for t in range(2)
    ]
    tile_rows = lax.broadcasted_iota(jnp.int32, (T, G * T), 0)
    tile_cols = lax.broadcasted_iota(jnp.int32, (T, G * T), 1)
    causal = tile_rows <= lax.rem(tile_cols, T)

    arrived(1)
    for h in range(HH):
        arrived(4 + h)

    def key_tile(h, which, b):
        slot, r = 2 - b // 2, b % 2
        if which == 0 and slot > 0:
            return kn[slot - 1, r * T : (r + 1) * T, :]
        return kv[slot, h, which, r * T : (r + 1) * T, :]

    away = (other, core)

    def g1(h, w, m):
        return remote(
            send1.at[h, w, half(m)], recv1.at[h, w, half(m)],
            g1_send.at[h, w, m], g1_recv.at[h, w, m], xn,
        )

    def g2(h, w, m):
        return remote(
            send2.at[h, w, half(m)], recv2.at[h, w, half(m)],
            g2_send.at[h, w, m], g2_recv.at[h, w, m], down,
        )

    def start_all(copy, *heads):
        for h in heads:
            for w in range(2):
                for m in away:
                    copy(h, w, m).start()

    def pass_down(h, w):
        @pl.when(par == 1)
        def _():
            for m in away:
                g1(h, w, m).wait_recv()
                total = part2[h, w, half(m)] + recv1[h, w, half(m)].astype(F32)
                send2[h, w, half(m)] = total.astype(BF16)

                @pl.when(has_down)
                def _():
                    g2(h, w, m).start()

    def fq(h):
        cols = pl.ds(pl.multiple_of(h * (G * HD), G * HD), G * HD)
        to = pl.ds(pl.multiple_of(core * QW + h * (G * HD), G * HD), G * HD)
        return (
            remote(dq.at[other, :, cols], out_q.at[:, to], fq_send.at[h], fq_recv.at[h], partner),
            pltpu.make_async_copy(dq.at[core, :, cols], out_q.at[:, to], fq_local.at[h]),
        )

    def fk_far(w, h):
        cols = pl.ds(pl.multiple_of(h * HD, HD), HD)
        to = pl.ds(pl.multiple_of(core * KW + h * HD, HD), HD)
        return remote(
            dkv.at[w, other, :, cols], (out_k, out_v)[w].at[:, to],
            fk_send.at[w, h], fk_recv.at[w, h], partner,
        )

    def fk_near(w, h):
        cols = pl.ds(pl.multiple_of(h * HD, HD), HD)
        to = pl.ds(pl.multiple_of(core * KW + h * HD, HD), HD)
        return pltpu.make_async_copy(
            dkv.at[w, core, :, cols], (out_k, out_v)[w].at[:, to], fk_local.at[w, h]
        )

    qg = qgain[...] * qk_scale
    own_at = {(0, 4): 0, (1, 4): 1, (1, 5): 2}

    def head_cols(h, g):
        return pl.ds(pl.multiple_of((h * G + g) * HD, HD), HD)

    def forward(h, t, b, q):
        s = dot(key_tile(h, 0, b), q, (1, 1))
        seen = tile_rows >= low_rows[t] - b * T
        if b == t + per - 1:
            seen = seen & causal
        e = jnp.where(seen, jnp.exp(s), 0.0)
        eb = e.astype(BF16)
        return eb, jnp.sum(e, axis=0, keepdims=True), dot(key_tile(h, 1, b), eb, (0, 0))

    def backward(h, b, ebs):
        dk = dv = None
        terms = {}
        for t, eb in ebs.items():
            dp = dot(key_tile(h, 1, b), gn[h, t], (1, 1))
            ds = (eb.astype(F32) * (dp - drow[h, t])).astype(BF16)
            dv_t = dot(eb, gn[h, t], (1, 0))
            dk_t = dot(ds, qn[h, t], (1, 0))
            dk = dk_t if dk is None else dk + dk_t
            dv = dv_t if dv is None else dv + dv_t
            terms[t] = dot(key_tile(h, 0, b), ds, (0, 0))
        return dk, dv, terms

    def own_forward(h, carry):
        for t in range(2):
            qn[h, t] = jnp.concatenate(
                [
                    (x * inverse_rms(x) * qg).astype(BF16)
                    for x in (
                        qx[t * T : (t + 1) * T, head_cols(h, g)].astype(F32) for g in range(G)
                    )
                ],
                axis=0,
            )
            total, o_t = 0.0, 0.0
            for b in (4, 5)[: t + 1]:
                eb, part, o_part = forward(h, t, b, qn[h, t])
                eown[h, own_at[t, b]] = eb
                total, o_t = total + part, o_t + o_part
            lsum[h, t] = total
            osum[h, t] = o_t

        for i, at in enumerate(((0, other), (1, core), (1, other))):

            @pl.when(h == i)
            def _():
                take_up(0, *at)

        return carry

    lax.fori_loop(0, HH, own_forward, 0)
    arrived(2)

    def head(h, carry):
        @pl.when((par == 0) & has_down)
        def _():
            for w in range(2):
                for s in range(2):
                    to_up(h, w, s, s).wait_recv()

        @pl.when(h == HH - 1)
        def _():
            for w in range(2):
                pass_down(0, w)

        for w in range(2):
            for s in range(2):
                relay(h, w, s).wait_recv()
        for slot in (1, 2):
            x = kv[slot, h, 0].astype(F32)
            kn[slot - 1] = (x * inverse_rms(x) * kgain[...]).astype(BF16)
        for t in range(2):
            total, o_t = lsum[h, t], osum[h, t]
            for b in range(t, 4):
                eb, part, o_part = forward(h, t, b, qn[h, t])
                efar[t, b] = eb
                total, o_t = total + part, o_t + o_part
            inv = 1.0 / total
            grads = [gx[t * T : (t + 1) * T, head_cols(h, g)].astype(F32) for g in range(G)]
            g_t = jnp.concatenate(grads, axis=0).T * inv
            drow[h, t] = jnp.sum(g_t.astype(BF16).astype(F32) * o_t, axis=0, keepdims=True) * inv
            gn[h, t] = g_t.T.astype(BF16)

            if t == 0:

                @pl.when(h + 1 < HH)
                def _():
                    take_up(h + 1, 0, core)

        @pl.when(h + 1 < HH)
        def _():
            take_up(h + 1, 0, other)

        @pl.when((par == 0) & has_down & (h == HH - 2))
        def _():
            start_all(g2, *range(HH - 2))

        dq_t = [0.0, 0.0]
        for b in (2, 3):
            dk, dv, terms = backward(h, b, {t: efar[t, b] for t in range(2)})
            at = slice((b - 2) * T, (b - 1) * T)
            send1[h, 0, at] = dk.astype(BF16)
            send1[h, 1, at] = dv.astype(BF16)
            for t in terms:
                dq_t[t] = dq_t[t] + terms[t]

        @pl.when((par == 0) | (h == HH - 1))
        def _():
            start_all(g1, h)

        @pl.when((par == 0) & (h == 0))
        def _():
            for w in range(2):
                for j in both:
                    to_xn(HH - 1, w, j, core).start()

        @pl.when(h == HH - 1)
        def _():
            pass_down(1, 0)

        @pl.when(h + 1 < HH)
        def _():
            take_up(h + 1, 1, core)

        for b in (0, 1):
            dk, dv, terms = backward(h, b, {t: efar[t, b] for t in range(b + 1)})
            at = slice(b * T, (b + 1) * T)
            part2[h, 0, at] = dk
            part2[h, 1, at] = dv
            for t in terms:
                dq_t[t] = dq_t[t] + terms[t]
        for t in range(2):
            dqsum[h, t] = dq_t[t]

        @pl.when((par == 0) & has_down)
        def _():
            for w in range(2):
                send2[h, w] = part2[h, w].astype(BF16)

            @pl.when(h >= HH - 2)
            def _():
                start_all(g2, h)

        @pl.when(h + 1 < HH)
        def _():
            take_up(h + 1, 1, other)

        for at, ready in ((HH - 3, range(HH - 3)), (HH - 2, range(HH - 3, HH - 1))):

            @pl.when((par == 1) & (h == at))
            def _():
                start_all(g1, *ready)

        return carry

    lax.fori_loop(0, HH, head, 0)

    def own_backward(h, carry):
        dq_t = [dqsum[h, 0], dqsum[h, 1]]
        for b in (4, 5):
            dk, dv, terms = backward(
                h, b, {t: eown[h, own_at[t, b]] for t in range(b - 4, 2)}
            )
            at = slice((b - 4) * T, (b - 3) * T)
            part0[h, 0, at] = dk
            part0[h, 1, at] = dv
            for t in terms:
                dq_t[t] = dq_t[t] + terms[t]
        for t in range(2):
            dqn = dq_t[t].T
            for g in range(G):
                x = qx[t * T : (t + 1) * T, head_cols(h, g)].astype(F32)
                dq[t, :, head_cols(h, g)] = norm_back(
                    x, inverse_rms(x), qg, dqn[g * T : (g + 1) * T]
                ).astype(BF16)
        far, near = fq(h)
        far.start()
        near.start()

        for i, at in ((0, (1, 1)), (2, (2, 0))):

            @pl.when(h == i)
            def _():
                pass_down(*at)

        return carry

    lax.fori_loop(0, HH, own_backward, 0)
    pass_down(2, 1)
    for i in range(3, HH):
        for w in range(2):
            pass_down(i, w)

    def finish(h, carry):
        cols = pl.ds(pl.multiple_of(h * HD, HD), HD)
        for w in range(2):
            for m, out in ((other, fk_far), (core, fk_near)):

                @pl.when(has_up)
                def _():
                    g2(h, w, m).wait_recv()

                @pl.when(par == 0)
                def _():
                    g1(h, w, m).wait_recv()

                d = part0[h, w, half(m)] + recv2[h, w, half(m)].astype(F32)
                d = d + jnp.where(par == 0, recv1[h, w, half(m)].astype(F32), 0.0)
                if w == 0:
                    x = kx[half(m), cols].astype(F32)
                    d = norm_back(x, inverse_rms(x), kgain[...], d)
                dkv[w, m, :, cols] = d.astype(BF16)
                out(w, h).start()
        return carry

    lax.fori_loop(0, HH, finish, 0)

    for rc, lc in swaps:
        rc.wait_send()

    for s in range(2):
        doc_xn(s, s).wait_send()

        @pl.when(has_up)
        def _():
            doc_up(s, s).wait_send()

    def drain(h, carry):
        for w in range(2):
            for s in range(2):
                to_xn(h, w, s, s).wait_send()
                g1(h, w, s).wait_send()

        @pl.when(has_up)
        def _():
            for w in range(2):
                for s in range(2):
                    to_up(h, w, s, s).wait_send()

        @pl.when(has_down)
        def _():
            for w in range(2):
                for m in range(2):
                    g2(h, w, m).wait_send()

        for far, near in (fq(h), (fk_far(0, h), fk_near(0, h)), (fk_far(1, h), fk_near(1, h))):
            far.wait_send()
            far.wait_recv()
            near.wait()
        return carry

    lax.fori_loop(0, HH, drain, 0)


def on_device(n, queries, keys, values, out_grad, q_gain, k_gain, doc_ids):
    T = queries.shape[0]
    kv_heads = keys.shape[1] // HD
    HH = kv_heads // 2
    G = queries.shape[1] // keys.shape[1]
    C = 2 * T
    per = WINDOW // T + 1
    doc_tile = (-(-doc_ids.shape[0] // 8) * 8, HD)
    DMA = pltpu.SemaphoreType.DMA
    vmem = pl.BlockSpec(memory_space=pltpu.VMEM)
    anywhere = pl.BlockSpec(memory_space=pltpu.HBM)
    scratch = [
        pltpu.VMEM((C, HH * G * HD), BF16),
        pltpu.VMEM((C, HH * G * HD), BF16),
        pltpu.VMEM((C, HH * HD), BF16),
        pltpu.VMEM(doc_tile, jnp.int32),
        pltpu.VMEM((3, 2) + doc_tile, jnp.int32),
        pltpu.VMEM((3, HH, 2, C, HD), BF16),
        pltpu.VMEM((2, C, HD), BF16),
        pltpu.VMEM((2, per - 1, T, G * T), BF16),
        pltpu.VMEM((HH, 3, T, G * T), BF16),
        pltpu.VMEM((HH, 2, G * T, HD), BF16),
        pltpu.VMEM((HH, 2, G * T, HD), BF16),
        pltpu.VMEM((HH, 2, 1, G * T), F32),
        pltpu.VMEM((HH, 2, HD, G * T), F32),
        pltpu.VMEM((HH, 2, 1, G * T), F32),
        pltpu.VMEM((HH, 2, HD, G * T), F32),
        pltpu.VMEM((HH, 2, C, HD), F32),
        pltpu.VMEM((HH, 2, C, HD), F32),
        pltpu.VMEM((HH, 2, C, HD), BF16),
        pltpu.VMEM((HH, 2, C, HD), BF16),
        pltpu.VMEM((HH, 2, C, HD), BF16),
        pltpu.VMEM((HH, 2, C, HD), BF16),
        pltpu.VMEM((2, T, HH * G * HD), BF16),
        pltpu.VMEM((2, 2, T, HH * HD), BF16),
        DMA((4 + HH,)), DMA((4 + HH,)), DMA((4 + HH,)), DMA((2,)), DMA((2,)), DMA((2,)), DMA((2,)),
        DMA((HH, 2, 2)), DMA((HH, 2, 2)), DMA((HH, 2, 2)), DMA((HH, 2, 2)),
        DMA((HH, 2, 2)), DMA((HH, 2, 2)), DMA((HH, 2, 2)), DMA((HH, 2, 2)),
        DMA((HH,)), DMA((HH,)), DMA((HH,)), DMA((2, HH)), DMA((2, HH)), DMA((2, HH)),
    ]
    return pl.pallas_call(
        functools.partial(kernel, n),
        out_shape=(
            pltpu.VMEM(queries.shape, BF16),
            pltpu.VMEM(keys.shape, BF16),
            pltpu.VMEM(values.shape, BF16),
        ),
        in_specs=[anywhere] * 4 + [vmem, vmem, pl.BlockSpec(memory_space=pltpu.SMEM)],
        out_specs=(vmem, vmem, vmem),
        scratch_shapes=scratch,
        compiler_params=pltpu.CompilerParams(
            collective_id=0, has_side_effects=True, vmem_limit_bytes=64700000
        ),
    )(queries, keys, values, out_grad, q_gain.reshape(1, HD), k_gain.reshape(1, HD), doc_ids)


def solution(mesh):
    split = P(("groups", "ctx"), None)
    return jax.shard_map(
        functools.partial(on_device, mesh.shape["ctx"]),
        mesh=mesh,
        in_specs=(split, split, split, split, P(), P(), P(("groups", "ctx"))),
        out_specs=(split, split, split),
        check_vma=False,
    )
```

```python
import functools

import jax
import jax.numpy as jnp
from jax import lax
from jax.experimental import pallas as pl
from jax.experimental.pallas import tpu as pltpu
from jax.sharding import PartitionSpec as P

HD = 128
WINDOW = 1024
BLK = 64

qk_scale = 168.0 ** (-0.5)
norm_epsilon = 1e-06

F32 = jnp.float32
BF16 = jnp.bfloat16


def dot(a, b, contract):
    return lax.dot_general(
        a, b, (((contract[0],), (contract[1],)), ((), ())), preferred_element_type=F32
    )


def inverse_rms(x):
    return lax.rsqrt(jnp.mean(x * x, axis=-1, keepdims=True) + norm_epsilon)


def norm_back(x, r, gain, incoming):
    scaled = incoming * gain
    return r * scaled - x * (r * r * r) * jnp.mean(x * scaled, axis=-1, keepdims=True)


def kernel(
    n, q_in, k_in, v_in, g_in, qgain, kgain, docs_in,
    out_q, out_k, out_v,
    qx, gx, kx, docs_own, docs, kv, kn, efar, eown, qn, gn, lsum, osum, drow, dqsum, part0, part2,
    send1, send2, recv1, recv2, dq, dkv,
    x_local, x_send, x_recv, du_send, du_recv, dx_send, dx_recv,
    up_send, up_recv, xn_send, xn_recv,
    g1_send, g1_recv, g2_send, g2_recv,
    fq_local, fq_send, fq_recv, fk_local, fk_send, fk_recv,
):
    T = q_in.shape[0]
    HH = kv.shape[1]
    G = q_in.shape[1] // k_in.shape[1]
    QW = HH * G * HD
    KW = HH * HD
    C = 2 * T
    per = WINDOW // T + 1

    me = lax.axis_index("ctx")
    core = lax.rem(me, 2)
    other = 1 - core
    chip = me // 2
    par = lax.rem(chip, 2)
    partner = me + 1 - 2 * core
    xn = me + 2 - 4 * par
    has_up, has_down = chip < n // 2 - 2, chip >= 2
    up = lax.rem(me + 4, n)
    down = lax.rem(me + n - 4, n)

    barrier = pltpu.get_barrier_semaphore()
    flip = 1 - 2 * core

    def greet(*peers):
        for who in peers:
            pl.semaphore_signal(
                barrier, inc=1, device_id={"ctx": who}, device_id_type=pl.DeviceIdType.MESH
            )

    @pl.when(has_up)
    def _():
        greet(up, up + flip)

    @pl.when(has_down)
    def _():
        greet(down, down + flip)

    greet(xn, xn + flip, partner)

    def remote(src, dst, s, r, who):
        return pltpu.make_async_remote_copy(
            src_ref=src, dst_ref=dst, send_sem=s, recv_sem=r,
            device_id={"ctx": who}, device_id_type=pl.DeviceIdType.MESH,
        )

    def half(c):
        return pl.ds(pl.multiple_of(c * T, T), T)

    rows = half(core)
    for b in range(docs_in.shape[0]):
        docs_own[b : b + 1, :] = jnp.full((1, HD), docs_in[b], jnp.int32)

    def part(who, width, at=0, size=None):
        size = width if size is None else size
        return pl.ds(pl.multiple_of(who * width + at, size), size)

    def swap(src, dst, i, mine, theirs):
        rc = remote(src.at[:, theirs], dst, x_send.at[i], x_recv.at[i], partner)
        lc = pltpu.make_async_copy(src.at[:, mine], dst, x_local.at[i])
        return rc, lc

    swaps = [
        swap(k_in, kx.at[rows, :], 0, part(core, KW), part(other, KW)),
        swap(q_in, qx.at[rows, :], 1, part(core, QW), part(other, QW)),
        swap(g_in, gx.at[rows, :], 2, part(core, QW), part(other, QW)),
        (
            remote(docs_own, docs.at[0, core], x_send.at[3], x_recv.at[3], partner),
            pltpu.make_async_copy(docs_own, docs.at[0, core], x_local.at[3]),
        ),
    ] + [
        swap(
            v_in, kv.at[0, h, 1, rows, :], 4 + h,
            part(core, KW, h * HD, HD), part(other, KW, h * HD, HD),
        )
        for h in range(HH)
    ]
    order = (3, 0, 4, 1, 5, 6, 7, 2) if HH == 4 else tuple(range(len(swaps)))

    def arrived(i):
        swaps[i][0].wait_recv()
        swaps[i][1].wait()

    def reach(who, c):
        return who + (c - core)

    def to_up(h, w, j, s):
        src = (k_in, v_in)[w].at[:, part(j, KW, h * HD, HD)]
        return remote(
            src, kv.at[2, h, w, half(s), :], up_send.at[h, w, j], up_recv.at[h, w, s],
            reach(up, j),
        )

    def to_xn(h, w, j, s):
        src = (k_in, v_in)[w].at[:, part(j, KW, h * HD, HD)]
        return remote(
            src, kv.at[1, h, w, half(s), :], xn_send.at[h, w, j], xn_recv.at[h, w, s],
            reach(xn, j),
        )

    def relay(h, w, s):
        return remote(
            kv.at[2, h, w, half(s), :], kv.at[1, h, w, half(s), :],
            xn_send.at[h, w, s], xn_recv.at[h, w, s], xn,
        )

    def doc_up(j, s):
        return remote(docs_own, docs.at[2, s], du_send.at[j], du_recv.at[s], reach(up, j))

    def doc_xn(j, s):
        return remote(docs_own, docs.at[1, s], dx_send.at[j], dx_recv.at[s], reach(xn, j))

    def doc_relay(s):
        return remote(docs.at[2, s], docs.at[1, s], dx_send.at[s], dx_recv.at[s], xn)

    for i in order:
        swaps[i][1].start()

    pl.semaphore_wait(barrier, 3 + 2 * jnp.where(has_up, 1, 0) + 2 * jnp.where(has_down, 1, 0))

    both = (core, other)
    swaps[3][0].start()

    @pl.when(has_up)
    def _():
        for j in both:
            doc_up(j, core).start()

    @pl.when(par == 0)
    def _():
        for j in both:
            doc_xn(j, core).start()

    for h in range(HH):

        @pl.when(has_up)
        def _():
            for w in range(2):
                for j in both:
                    to_up(h, w, j, core).start()

        if h < HH - 1:

            @pl.when(par == 0)
            def _():
                for w in range(2):
                    for j in both:
                        to_xn(h, w, j, core).start()

    for i in order[1:]:
        swaps[i][0].start()

    @pl.when(chip < 2)
    def _():
        kv[2] = jnp.zeros(kv.shape[1:], BF16)
        docs[2] = jnp.zeros(docs.shape[1:], jnp.int32)

    @pl.when(chip >= n // 2 - 2)
    def _():
        recv2[...] = jnp.zeros(recv2.shape, BF16)

    arrived(3)
    for s in both:

        @pl.when(has_down)
        def _():
            doc_up(s, s).wait_recv()

        @pl.when(par == 1)
        def _():
            doc_relay(s).start()

    def take_up(h, w, *sides):
        @pl.when(par == 1)
        def _():
            for s in sides:

                @pl.when(has_down)
                def _():
                    to_up(h, w, s, s).wait_recv()

                relay(h, w, s).start()

    take_up(0, 0, core)
    arrived(0)

    for h in range(HH):
        x = kx[:, h * HD : (h + 1) * HD].astype(F32)
        kv[0, h, 0] = (x * inverse_rms(x) * kgain[...]).astype(BF16)

    for s in range(2):
        doc_xn(s, s).wait_recv()

    lane = lax.broadcasted_iota(jnp.int32, (1, HD), 1)
    blocks = T // BLK
    qdocs = []
    for m in range(2):
        for b in range(0, blocks, 2):
            qdocs.append(
                jnp.where(lane < BLK, docs[0, m, b : b + 1, :], docs[0, m, b + 1 : b + 2, :])
            )
    lows = []
    for i, qd in enumerate(qdocs):
        low = jnp.zeros((1, HD), jnp.int32)
        for slot in (2, 1, 0):
            for m in range(2):
                for b in range(blocks):
                    kd = jnp.where(chip >= slot, docs[slot, m, b : b + 1, :], -1)
                    low = low + jnp.where(kd < qd, BLK, 0)
        lows.append(jnp.maximum(low, lane + (i * HD + 1)))
    hl = len(lows) // 2
    low_rows = [
        jnp.concatenate([x for _ in range(G) for x in lows[t * hl : (t + 1) * hl]], axis=1)
        for t in range(2)
    ]
    tile_rows = lax.broadcasted_iota(jnp.int32, (T, G * T), 0)
    tile_cols = lax.broadcasted_iota(jnp.int32, (T, G * T), 1)
    causal = tile_rows <= lax.rem(tile_cols, T)

    arrived(1)
    for h in range(HH):
        arrived(4 + h)

    def key_tile(h, which, b):
        slot, r = 2 - b // 2, b % 2
        if which == 0 and slot > 0:
            return kn[slot - 1, r * T : (r + 1) * T, :]
        return kv[slot, h, which, r * T : (r + 1) * T, :]

    away = (other, core)

    def g1(h, w, m):
        return remote(
            send1.at[h, w, half(m)], recv1.at[h, w, half(m)],
            g1_send.at[h, w, m], g1_recv.at[h, w, m], xn,
        )

    def g2(h, w, m):
        return remote(
            send2.at[h, w, half(m)], recv2.at[h, w, half(m)],
            g2_send.at[h, w, m], g2_recv.at[h, w, m], down,
        )

    def start_all(copy, *heads):
        for h in heads:
            for w in range(2):
                for m in away:
                    copy(h, w, m).start()

    def pass_down(h, w):
        @pl.when(par == 1)
        def _():
            for m in away:
                g1(h, w, m).wait_recv()
                total = part2[h, w, half(m)] + recv1[h, w, half(m)].astype(F32)
                send2[h, w, half(m)] = total.astype(BF16)

                @pl.when(has_down)
                def _():
                    g2(h, w, m).start()

    def fq(h):
        cols = pl.ds(pl.multiple_of(h * (G * HD), G * HD), G * HD)
        to = pl.ds(pl.multiple_of(core * QW + h * (G * HD), G * HD), G * HD)
        return (
            remote(dq.at[other, :, cols], out_q.at[:, to], fq_send.at[h], fq_recv.at[h], partner),
            pltpu.make_async_copy(dq.at[core, :, cols], out_q.at[:, to], fq_local.at[h]),
        )

    def fk_far(w, h):
        cols = pl.ds(pl.multiple_of(h * HD, HD), HD)
        to = pl.ds(pl.multiple_of(core * KW + h * HD, HD), HD)
        return remote(
            dkv.at[w, other, :, cols], (out_k, out_v)[w].at[:, to],
            fk_send.at[w, h], fk_recv.at[w, h], partner,
        )

    def fk_near(w, h):
        cols = pl.ds(pl.multiple_of(h * HD, HD), HD)
        to = pl.ds(pl.multiple_of(core * KW + h * HD, HD), HD)
        return pltpu.make_async_copy(
            dkv.at[w, core, :, cols], (out_k, out_v)[w].at[:, to], fk_local.at[w, h]
        )

    qg = qgain[...] * qk_scale
    own_at = {(0, 4): 0, (1, 4): 1, (1, 5): 2}

    def head_cols(h, g):
        return pl.ds(pl.multiple_of((h * G + g) * HD, HD), HD)

    def forward(h, t, b, q):
        s = dot(key_tile(h, 0, b), q, (1, 1))
        seen = tile_rows >= low_rows[t] - b * T
        if b == t + per - 1:
            seen = seen & causal
        e = jnp.where(seen, jnp.exp(s), 0.0)
        eb = e.astype(BF16)
        return eb, jnp.sum(e, axis=0, keepdims=True), dot(key_tile(h, 1, b), eb, (0, 0))

    def backward(h, b, ebs):
        dk = dv = None
        terms = {}
        for t, eb in ebs.items():
            dp = dot(key_tile(h, 1, b), gn[h, t], (1, 1))
            ds = (eb.astype(F32) * (dp - drow[h, t])).astype(BF16)
            dv_t = dot(eb, gn[h, t], (1, 0))
            dk_t = dot(ds, qn[h, t], (1, 0))
            dk = dk_t if dk is None else dk + dk_t
            dv = dv_t if dv is None else dv + dv_t
            terms[t] = dot(key_tile(h, 0, b), ds, (0, 0))
        return dk, dv, terms

    def own_forward(h, carry):
        for t in range(2):
            qn[h, t] = jnp.concatenate(
                [
                    (x * inverse_rms(x) * qg).astype(BF16)
                    for x in (
                        qx[t * T : (t + 1) * T, head_cols(h, g)].astype(F32) for g in range(G)
                    )
                ],
                axis=0,
            )
            total, o_t = 0.0, 0.0
            for b in (4, 5)[: t + 1]:
                eb, part, o_part = forward(h, t, b, qn[h, t])
                eown[h, own_at[t, b]] = eb
                total, o_t = total + part, o_t + o_part
            lsum[h, t] = total
            osum[h, t] = o_t

        for i, at in enumerate(((0, other), (1, core), (1, other))):

            @pl.when(h == i)
            def _():
                take_up(0, *at)

        return carry

    lax.fori_loop(0, HH, own_forward, 0)
    arrived(2)

    def head(h, carry):
        @pl.when((par == 0) & has_down)
        def _():
            for w in range(2):
                for s in range(2):
                    to_up(h, w, s, s).wait_recv()

        @pl.when(h == HH - 1)
        def _():
            for w in range(2):
                pass_down(0, w)

        for w in range(2):
            for s in range(2):
                relay(h, w, s).wait_recv()
        for slot in (1, 2):
            x = kv[slot, h, 0].astype(F32)
            kn[slot - 1] = (x * inverse_rms(x) * kgain[...]).astype(BF16)
        for t in range(2):
            total, o_t = lsum[h, t], osum[h, t]
            for b in range(t, 4):
                eb, part, o_part = forward(h, t, b, qn[h, t])
                efar[t, b] = eb
                total, o_t = total + part, o_t + o_part
            inv = 1.0 / total
            grads = [gx[t * T : (t + 1) * T, head_cols(h, g)].astype(F32) for g in range(G)]
            g_t = jnp.concatenate(grads, axis=0).T * inv
            drow[h, t] = jnp.sum(g_t.astype(BF16).astype(F32) * o_t, axis=0, keepdims=True) * inv
            gn[h, t] = g_t.T.astype(BF16)

            if t == 0:

                @pl.when(h + 1 < HH)
                def _():
                    take_up(h + 1, 0, core)

        @pl.when(h + 1 < HH)
        def _():
            take_up(h + 1, 0, other)

        @pl.when((par == 0) & has_down & (h == HH - 2))
        def _():
            start_all(g2, *range(HH - 2))

        dq_t = [0.0, 0.0]
        for b in (2, 3):
            dk, dv, terms = backward(h, b, {t: efar[t, b] for t in range(2)})
            at = slice((b - 2) * T, (b - 1) * T)
            send1[h, 0, at] = dk.astype(BF16)
            send1[h, 1, at] = dv.astype(BF16)
            for t in terms:
                dq_t[t] = dq_t[t] + terms[t]

        @pl.when((par == 0) | (h == HH - 1))
        def _():
            start_all(g1, h)

        @pl.when((par == 0) & (h == 0))
        def _():
            for w in range(2):
                for j in both:
                    to_xn(HH - 1, w, j, core).start()

        @pl.when(h == HH - 1)
        def _():
            pass_down(1, 0)

        @pl.when(h + 1 < HH)
        def _():
            take_up(h + 1, 1, core)

        for b in (0, 1):
            dk, dv, terms = backward(h, b, {t: efar[t, b] for t in range(b + 1)})
            at = slice(b * T, (b + 1) * T)
            part2[h, 0, at] = dk
            part2[h, 1, at] = dv
            for t in terms:
                dq_t[t] = dq_t[t] + terms[t]
        for t in range(2):
            dqsum[h, t] = dq_t[t]

        @pl.when((par == 0) & has_down)
        def _():
            for w in range(2):
                send2[h, w] = part2[h, w].astype(BF16)

            @pl.when(h >= HH - 2)
            def _():
                start_all(g2, h)

        @pl.when(h + 1 < HH)
        def _():
            take_up(h + 1, 1, other)

        for at, ready in ((HH - 3, range(HH - 3)), (HH - 2, range(HH - 3, HH - 1))):

            @pl.when((par == 1) & (h == at))
            def _():
                start_all(g1, *ready)

        return carry

    lax.fori_loop(0, HH, head, 0)

    def own_backward(h, carry):
        dq_t = [dqsum[h, 0], dqsum[h, 1]]
        for b in (4, 5):
            dk, dv, terms = backward(
                h, b, {t: eown[h, own_at[t, b]] for t in range(b - 4, 2)}
            )
            at = slice((b - 4) * T, (b - 3) * T)
            part0[h, 0, at] = dk
            part0[h, 1, at] = dv
            for t in terms:
                dq_t[t] = dq_t[t] + terms[t]
        for t in range(2):
            dqn = dq_t[t].T
            for g in range(G):
                x = qx[t * T : (t + 1) * T, head_cols(h, g)].astype(F32)
                dq[t, :, head_cols(h, g)] = norm_back(
                    x, inverse_rms(x), qg, dqn[g * T : (g + 1) * T]
                ).astype(BF16)
        far, near = fq(h)
        far.start()
        near.start()

        for i, at in ((0, (1, 1)), (2, (2, 0))):

            @pl.when(h == i)
            def _():
                pass_down(*at)

        return carry

    lax.fori_loop(0, HH, own_backward, 0)
    pass_down(2, 1)
    for i in range(3, HH):
        for w in range(2):
            pass_down(i, w)

    def finish(h, carry):
        cols = pl.ds(pl.multiple_of(h * HD, HD), HD)
        for w in range(2):
            for m, out in ((other, fk_far), (core, fk_near)):

                @pl.when(has_up)
                def _():
                    g2(h, w, m).wait_recv()

                @pl.when(par == 0)
                def _():
                    g1(h, w, m).wait_recv()

                d = part0[h, w, half(m)] + recv2[h, w, half(m)].astype(F32)
                d = d + jnp.where(par == 0, recv1[h, w, half(m)].astype(F32), 0.0)
                if w == 0:
                    x = kx[half(m), cols].astype(F32)
                    d = norm_back(x, inverse_rms(x), kgain[...], d)
                dkv[w, m, :, cols] = d.astype(BF16)
                out(w, h).start()
        return carry

    lax.fori_loop(0, HH, finish, 0)

    for rc, lc in swaps:
        rc.wait_send()

    for s in range(2):
        doc_xn(s, s).wait_send()

        @pl.when(has_up)
        def _():
            doc_up(s, s).wait_send()

    def drain(h, carry):
        for w in range(2):
            for s in range(2):
                to_xn(h, w, s, s).wait_send()
                g1(h, w, s).wait_send()

        @pl.when(has_up)
        def _():
            for w in range(2):
                for s in range(2):
                    to_up(h, w, s, s).wait_send()

        @pl.when(has_down)
        def _():
            for w in range(2):
                for m in range(2):
                    g2(h, w, m).wait_send()

        for far, near in (fq(h), (fk_far(0, h), fk_near(0, h)), (fk_far(1, h), fk_near(1, h))):
            far.wait_send()
            far.wait_recv()
            near.wait()
        return carry

    lax.fori_loop(0, HH, drain, 0)


def put_out(a, b, c, out_a, out_b, out_c, sems):
    copies = [
        pltpu.make_async_copy(src, dst, sems.at[i])
        for i, (src, dst) in enumerate(((a, out_a), (b, out_b), (c, out_c)))
    ]
    for copy in copies:
        copy.start()
    for copy in copies:
        copy.wait()


def on_device(n, queries, keys, values, out_grad, q_gain, k_gain, doc_ids):
    T = queries.shape[0]
    kv_heads = keys.shape[1] // HD
    HH = kv_heads // 2
    G = queries.shape[1] // keys.shape[1]
    C = 2 * T
    per = WINDOW // T + 1
    doc_tile = (-(-doc_ids.shape[0] // 8) * 8, HD)
    DMA = pltpu.SemaphoreType.DMA
    vmem = pl.BlockSpec(memory_space=pltpu.VMEM)
    anywhere = pl.BlockSpec(memory_space=pltpu.HBM)
    scratch = [
        pltpu.VMEM((C, HH * G * HD), BF16),
        pltpu.VMEM((C, HH * G * HD), BF16),
        pltpu.VMEM((C, HH * HD), BF16),
        pltpu.VMEM(doc_tile, jnp.int32),
        pltpu.VMEM((3, 2) + doc_tile, jnp.int32),
        pltpu.VMEM((3, HH, 2, C, HD), BF16),
        pltpu.VMEM((2, C, HD), BF16),
        pltpu.VMEM((2, per - 1, T, G * T), BF16),
        pltpu.VMEM((HH, 3, T, G * T), BF16),
        pltpu.VMEM((HH, 2, G * T, HD), BF16),
        pltpu.VMEM((HH, 2, G * T, HD), BF16),
        pltpu.VMEM((HH, 2, 1, G * T), F32),
        pltpu.VMEM((HH, 2, HD, G * T), F32),
        pltpu.VMEM((HH, 2, 1, G * T), F32),
        pltpu.VMEM((HH, 2, HD, G * T), F32),
        pltpu.VMEM((HH, 2, C, HD), F32),
        pltpu.VMEM((HH, 2, C, HD), F32),
        pltpu.VMEM((HH, 2, C, HD), BF16),
        pltpu.VMEM((HH, 2, C, HD), BF16),
        pltpu.VMEM((HH, 2, C, HD), BF16),
        pltpu.VMEM((HH, 2, C, HD), BF16),
        pltpu.VMEM((2, T, HH * G * HD), BF16),
        pltpu.VMEM((2, 2, T, HH * HD), BF16),
        DMA((4 + HH,)), DMA((4 + HH,)), DMA((4 + HH,)), DMA((2,)), DMA((2,)), DMA((2,)), DMA((2,)),
        DMA((HH, 2, 2)), DMA((HH, 2, 2)), DMA((HH, 2, 2)), DMA((HH, 2, 2)),
        DMA((HH, 2, 2)), DMA((HH, 2, 2)), DMA((HH, 2, 2)), DMA((HH, 2, 2)),
        DMA((HH,)), DMA((HH,)), DMA((HH,)), DMA((2, HH)), DMA((2, HH)), DMA((2, HH)),
    ]
    grads = pl.pallas_call(
        functools.partial(kernel, n),
        out_shape=(
            pltpu.VMEM(queries.shape, BF16),
            pltpu.VMEM(keys.shape, BF16),
            pltpu.VMEM(values.shape, BF16),
        ),
        in_specs=[anywhere] * 4 + [vmem, vmem, pl.BlockSpec(memory_space=pltpu.SMEM)],
        out_specs=(vmem, vmem, vmem),
        scratch_shapes=scratch,
        compiler_params=pltpu.CompilerParams(
            collective_id=0, has_side_effects=True, vmem_limit_bytes=64700000
        ),
    )(queries, keys, values, out_grad, q_gain.reshape(1, HD), k_gain.reshape(1, HD), doc_ids)
    return pl.pallas_call(
        put_out,
        out_shape=tuple(jax.ShapeDtypeStruct(x.shape, BF16) for x in (queries, keys, values)),
        in_specs=[pl.BlockSpec(memory_space=pl.ANY)] * 3,
        out_specs=(anywhere, anywhere, anywhere),
        scratch_shapes=[DMA((3,))],
        compiler_params=pltpu.CompilerParams(vmem_limit_bytes=1 << 20),
    )(*grads)


def solution(mesh):
    split = P(("groups", "ctx"), None)
    return jax.shard_map(
        functools.partial(on_device, mesh.shape["ctx"]),
        mesh=mesh,
        in_specs=(split, split, split, split, P(), P(), P(("groups", "ctx"))),
        out_specs=(split, split, split),
        check_vma=False,
    )
```
